32 devices in a mesh: section: 2 (over y), dp: 4 (over z), tensor: 4 (over x, core).
Axes of the slice: x: 2, y: 2, z: 4, core: 2. Of those that a mesh axis runs over, the one named last changes fastest.
Arguments:
- tokens: bfloat16 [2048, 1088], P(('dp', 'tensor')), may hold values from -6 to 6
- lengths: int32 [16, 2, 4], P(('dp', 'tensor')), may hold values from 1 to 42, 64 in all within a row
- w_qkv: bfloat16 [2, 1088, 3264], P('section'), may hold values from -2 to 2, as said below
- w_out: bfloat16 [2, 1088, 1088], P('section'), may hold values from -0.375 to 0.375
- w_up: bfloat16 [2, 1088, 4352], P('section', None, 'tensor'), may hold values from -0.1875 to 0.1875
- up_bias: float32 [2, 4352], P('section', 'tensor'), may hold values from -3 to 3
- w_down: bfloat16 [2, 4352, 1088], P('section', 'tensor'), may hold values from -0.09375 to 0.09375
- gains: float32 [2, 2, 1088], P('section'), may hold values from 0.25 to 1.75
- biases: float32 [2, 6, 1088], P('section'), may hold values from -2.5 to 2.5
- cotangent: bfloat16 [2048, 1088], P(('dp', 'tensor')), may hold values from -6 to 6
Outputs:
- layer_outputs: bfloat16 [2, 2048, 1088], P('section', ('dp', 'tensor'))
- input_grads: bfloat16 [2, 2048, 1088], P('section', ('dp', 'tensor'))
- grad_w_qkv: float32 [2, 1088, 3264], P('section', ('dp', 'tensor'))
- grad_w_out: float32 [2, 1088, 1088], P('section', ('dp', 'tensor'))
- grad_gains: float32 [2, 2, 1088], P('section', None, ('dp', 'tensor'))
- grad_biases: float32 [2, 6, 1088], P('section', None, ('dp', 'tensor'))
- grad_w_up: float32 [2, 1088, 4352], P('section', None, 'tensor')
- grad_up_bias: float32 [2, 4352], P('section', 'tensor')
- grad_w_down: float32 [2, 4352, 1088], P('section', 'tensor')
The draws below stay inside these ranges and needn't reach their ends.
Inputs may be any that keep to these rules, and one draw needn't show every extreme that they name: Each device's rows of one micro-batch hold 4 whole sequences whose lengths sum to 64; the longest is 42. `w_qkv`: columns are queries, keys and values in that order.
All inputs are finite; a program needn't handle non-finite values.
Results may differ from the reference program's by a relative error of at most 0.025.
Values may be sent and summed in bfloat16 or wider, within the bound.
A program may use at most 192 MiB of HBM per device.

```python
import math
import jax
import jax.numpy as jnp
import numpy as np
from jax import lax

D = 1088
HEADS = 17
HEAD_DIM = 64
FF = 4352
ROWS_MB = 64
MICRO = 2
SEQS = 4
DEV_ST = 16
TOKENS = 2048
N_TENSOR = 4


def draw_w_qkv(key, part):
    base = jnp.clip(jax.random.normal(key, (2, D, 3 * D), jnp.float32), -4.0, 4.0) * D ** (-0.5)
    return base.astype(jnp.bfloat16)


def level_of(stream_key, extent, cuts, low, largest):
    level = 1.0
    for position, parts in cuts:
        steps = jax.random.uniform(jax.random.fold_in(jax.random.fold_in(stream_key, 6), position), (parts,), jnp.float32, low / len(cuts), largest / len(cuts))
        level = level * jnp.repeat(jnp.exp(steps), extent[position] // parts).reshape((-1,) + (1,) * (len(extent) - 1 - position))
    return level


def profile(count, total, most, lean):
    weights = [(1 << 20) // math.isqrt(rank ** lean) + 1 for rank in range(2, count + 1)]
    rest, counts = total - most - (count - 1), [1] * (count - 1)
    while rest > 0:
        movable = [i for i in range(count - 1) if counts[i] < most]
        mass, left = sum([weights[i] for i in movable]), rest
        for i in movable:
            extra = min(most - counts[i], max(1, left * weights[i] // mass), rest)
            counts[i] = counts[i] + extra
            rest = rest - extra
    return np.array([most] + counts)


def ragged(own_key, amount, total, limit, slope):
    if amount == 2:
        one = jax.random.randint(own_key, (), max(1, total - limit), min(limit, total - 1) + 1)
        return jnp.stack([one, total - one])
    tallies = jnp.asarray(profile(amount, total, limit, slope), jnp.int32)
    couples = (amount - 1) // 2
    donor, receiver = tallies[1:1 + 2 * couples:2], tallies[2:2 + 2 * couples:2]
    margin = jnp.minimum(donor - 1, limit - receiver)
    moved = jax.random.randint(jax.random.fold_in(own_key, 1), (couples,), 0, 1 << 20) % (margin + 1)
    tallies = tallies.at[1:1 + 2 * couples:2].set(donor - moved).at[2:2 + 2 * couples:2].set(receiver + moved)
    return tallies[jax.random.permutation(jax.random.fold_in(own_key, 2), amount)]


def bell_draw(stream_key, dims, spread, reach, cuts=(), kind=jnp.bfloat16):
    level = level_of(stream_key, dims, cuts, -0.22, 0.18) if cuts else 1.0
    entries = jax.random.normal(stream_key, dims, jnp.float32) * spread * level
    return jnp.minimum(jnp.maximum(entries, -reach), reach).astype(kind)


def setup_inputs(seed: int = 0) -> dict:
    seeds = jax.random.split(jax.random.key(seed), 11)
    tokens = bell_draw(seeds[0], (TOKENS, D), 1.0, 6.0, ((0, 16),))
    lengths = jax.vmap(lambda own: ragged(own, SEQS, ROWS_MB, 2 * ROWS_MB // 3, 2))(jax.random.split(seeds[1], DEV_ST * MICRO)).reshape((DEV_ST, MICRO, SEQS)).astype(jnp.int32)
    w_qkv = draw_w_qkv(jax.random.fold_in(seeds[10], 71), 0)
    w_out = bell_draw(seeds[3], (2, D, D), (D // 4) ** -0.5, 0.375, ((0, 2),))
    w_up = bell_draw(seeds[4], (2, D, FF), D ** -0.5, 0.1875, ((0, 2), (2, 4)))
    up_bias = bell_draw(seeds[5], (2, FF), 0.5, 3.0, ((0, 2), (1, 4)), jnp.float32)
    w_down = bell_draw(seeds[6], (2, FF, D), FF ** -0.5, 0.09375, ((0, 2), (1, 4)))
    gains = jnp.clip(1.0 + 0.15 * jax.random.normal(seeds[7], (2, 2, D), jnp.float32), 0.25, 1.75)
    biases = bell_draw(seeds[8], (2, 6, D), 0.4, 2.5, ((0, 2),), jnp.float32)
    cotangent = bell_draw(seeds[9], (TOKENS, D), 1.0, 6.0, ((0, 16),))
    return {"tokens": tokens, "lengths": lengths, "w_qkv": w_qkv, "w_out": w_out, "w_up": w_up, "up_bias": up_bias, "w_down": w_down, "gains": gains, "biases": biases, "cotangent": cotangent}


EPSILON = 1e-05
GELU_SCALE = math.sqrt(2.0 / math.pi)
GELU_CUBIC = 0.044715

def norm_rows(values):
    centre = values - lax.optimization_barrier(jnp.mean(values, axis=-1, keepdims=True))
    inverse = lax.rsqrt(lax.optimization_barrier(jnp.mean(centre * centre, axis=-1, keepdims=True)) + EPSILON)
    return (centre * inverse, inverse)

def norm_back(grad_normed, normed, inverse, gain):
    scaled = grad_normed * gain
    return (scaled - lax.optimization_barrier(jnp.mean(scaled, axis=-1, keepdims=True)) - normed * lax.optimization_barrier(jnp.mean(scaled * normed, axis=-1, keepdims=True))) * inverse

def gelu_tanh(values):
    return 0.5 * values * (1.0 + jnp.tanh(GELU_SCALE * (values + GELU_CUBIC * values * values * values)))

def gelu_slope(values):
    tangent = jnp.tanh(GELU_SCALE * (values + GELU_CUBIC * values * values * values))
    return 0.5 * (1.0 + tangent) + 0.5 * values * (1.0 - tangent * tangent) * GELU_SCALE * (1.0 + 3.0 * GELU_CUBIC * values * values)

def contract_rows(left, right):
    return lax.dot_general(left, right, (((0,), (0,)), ((), ())), preferred_element_type=jnp.float32)

def contract_cols(left, right):
    return lax.dot_general(left, right, (((1,), (1,)), ((), ())), preferred_element_type=jnp.float32)

def make_allowed(seq_lengths):
    ends = jnp.cumsum(seq_lengths.astype(jnp.int32))
    places = jnp.arange(ROWS_MB, dtype=jnp.int32)
    segment = lax.optimization_barrier(jnp.sum((places[:, None] >= ends[None, :]).astype(jnp.int32), axis=1))
    return (segment[:, None] == segment[None, :]) & (places[None, :] <= places[:, None])

def round_trip(values):
    return lax.optimization_barrier(values.astype(jnp.bfloat16)).astype(jnp.float32)

def head_split(values):
    return values.reshape(ROWS_MB, HEADS, HEAD_DIM).astype(jnp.float32)

def scores_of(queries, keys_all, allowed):
    scores = jnp.einsum('qhd,khd->hqk', head_split(queries), head_split(keys_all), precision=lax.Precision.HIGHEST) * HEAD_DIM ** (-0.5)
    return jnp.where(allowed[None], scores, -jnp.inf)

def forward(layer_in, seq_lengths, params):
    w_qkv, w_out, w_up, up_bias, w_down, gains, biases, up_parts, down_parts = params
    allowed = make_allowed(seq_lengths)
    inflow = layer_in.astype(jnp.float32)
    normed_one, inverse_one = norm_rows(inflow)
    normal_one = (normed_one * gains[0] + biases[0]).astype(jnp.bfloat16)
    projected = jnp.dot(normal_one, w_qkv, preferred_element_type=jnp.float32)
    queries = (projected[:, :D] + biases[1]).astype(jnp.bfloat16)
    keys_all = projected[:, D:2 * D].astype(jnp.bfloat16)
    values_all = (projected[:, 2 * D:] + biases[2]).astype(jnp.bfloat16)
    masked = scores_of(queries, keys_all, allowed)
    peak = lax.optimization_barrier(jnp.max(masked, axis=-1, keepdims=True))
    log_total = peak + jnp.log(lax.optimization_barrier(jnp.sum(jnp.exp(masked - peak), axis=-1, keepdims=True)))
    probs = jnp.exp(masked - log_total).astype(jnp.bfloat16)
    mixed = jnp.einsum('hqk,khd->qhd', probs.astype(jnp.float32), head_split(values_all), precision=lax.Precision.HIGHEST)
    mixed = mixed.reshape(ROWS_MB, D).astype(jnp.bfloat16)
    residual = inflow + jnp.dot(mixed, w_out, preferred_element_type=jnp.float32) + biases[3]
    normed_two, inverse_two = norm_rows(residual)
    normal_two = (normed_two * gains[1] + biases[4]).astype(jnp.bfloat16)
    hidden_pre = jnp.dot(normal_two, w_up, preferred_element_type=jnp.float32) + up_bias
    hidden = gelu_tanh(hidden_pre).astype(jnp.bfloat16)
    pieces = jnp.einsum('rjf,jfd->jrd', hidden.reshape(ROWS_MB, N_TENSOR, FF // N_TENSOR).astype(jnp.float32), down_parts, precision=lax.Precision.HIGHEST)
    branch = lax.optimization_barrier(jnp.sum(round_trip(pieces), axis=0))
    result = (residual + branch + biases[5]).astype(jnp.bfloat16)
    kept = (allowed, normal_one, normed_one, inverse_one, queries, keys_all, values_all, mixed, log_total, normed_two, inverse_two, normal_two, hidden_pre, hidden)
    return (result, kept)

def backward(grad_out, kept, params):
    w_qkv, w_out, w_up, up_bias, w_down, gains, biases, up_parts, down_parts = params
    allowed, normal_one, normed_one, inverse_one, queries, keys_all, values_all, mixed, log_total, normed_two, inverse_two, normal_two, hidden_pre, hidden = kept
    grad_flow = grad_out.astype(jnp.float32)
    grad_down = contract_rows(hidden, grad_out)
    grad_hidden = contract_cols(grad_out, w_down)
    grad_pre = grad_hidden * gelu_slope(hidden_pre)
    grad_up_bias = lax.optimization_barrier(jnp.sum(grad_pre, axis=0))
    grad_pre_b = grad_pre.astype(jnp.bfloat16)
    grad_up = contract_rows(normal_two, grad_pre_b)
    pieces = jnp.einsum('rjf,djf->jrd', grad_pre_b.reshape(ROWS_MB, N_TENSOR, FF // N_TENSOR).astype(jnp.float32), up_parts, precision=lax.Precision.HIGHEST)
    grad_two = lax.optimization_barrier(jnp.sum(round_trip(pieces), axis=0))
    grad_resid = grad_flow + norm_back(grad_two, normed_two, inverse_two, gains[1])
    grad_resid_b = grad_resid.astype(jnp.bfloat16)
    grad_wout = contract_rows(mixed, grad_resid_b)
    grad_mixed = contract_cols(grad_resid_b, w_out).astype(jnp.bfloat16)
    masked = scores_of(queries, keys_all, allowed)
    probs_f = jnp.exp(masked - log_total)
    probs_b = probs_f.astype(jnp.bfloat16).astype(jnp.float32)
    grad_heads = head_split(grad_mixed)
    grad_probs = jnp.einsum('qhd,khd->hqk', grad_heads, head_split(values_all), precision=lax.Precision.HIGHEST)
    grad_values = jnp.einsum('hqk,qhd->khd', probs_b, grad_heads, precision=lax.Precision.HIGHEST).reshape(ROWS_MB, D)
    centre = lax.optimization_barrier(jnp.sum(probs_f * grad_probs, axis=-1, keepdims=True))
    grad_scores = (probs_f * (grad_probs - centre) * HEAD_DIM ** (-0.5)).astype(jnp.bfloat16).astype(jnp.float32)
    grad_queries = jnp.einsum('hqk,khd->qhd', grad_scores, head_split(keys_all), precision=lax.Precision.HIGHEST).reshape(ROWS_MB, D)
    grad_keys = jnp.einsum('hqk,qhd->khd', grad_scores, head_split(queries), precision=lax.Precision.HIGHEST).reshape(ROWS_MB, D)
    grad_proj = jnp.concatenate([grad_queries, grad_keys, grad_values], axis=1).astype(jnp.bfloat16)
    grad_wqkv = contract_rows(normal_one, grad_proj)
    grad_one = contract_cols(grad_proj, w_qkv)
    grad_in = (grad_resid + norm_back(grad_one, normed_one, inverse_one, gains[0])).astype(jnp.bfloat16)
    gain_grads = jnp.stack([lax.optimization_barrier(jnp.sum(normed_one * grad_one, axis=0)), lax.optimization_barrier(jnp.sum(normed_two * grad_two, axis=0))])
    bias_grads = jnp.stack([lax.optimization_barrier(jnp.sum(grad_one, axis=0)), lax.optimization_barrier(jnp.sum(grad_queries, axis=0)), lax.optimization_barrier(jnp.sum(grad_values, axis=0)), lax.optimization_barrier(jnp.sum(grad_resid, axis=0)), lax.optimization_barrier(jnp.sum(grad_two, axis=0)), lax.optimization_barrier(jnp.sum(grad_flow, axis=0))])
    return (grad_in, (grad_wqkv, grad_wout, gain_grads, bias_grads, grad_up, grad_down, grad_up_bias))

def layer_params(layer, w_qkv, w_out, w_up, up_bias, w_down, gains, biases):
    up_parts = w_up[layer].astype(jnp.float32).reshape(D, N_TENSOR, FF // N_TENSOR)
    down_parts = w_down[layer].astype(jnp.float32).reshape(N_TENSOR, FF // N_TENSOR, D)
    return (w_qkv[layer], w_out[layer], w_up[layer], up_bias[layer], w_down[layer], gains[layer], biases[layer], up_parts, down_parts)

def run_layer(inputs, cots, seq_table, params):
    zeros_init = (jnp.zeros((D, 3 * D), jnp.float32), jnp.zeros((D, D), jnp.float32), jnp.zeros((2, D), jnp.float32), jnp.zeros((6, D), jnp.float32), jnp.zeros((D, FF), jnp.float32), jnp.zeros((FF, D), jnp.float32), jnp.zeros((FF,), jnp.float32))

    def one_block(totals, block):
        block_in, block_cot, block_lengths = block
        result, kept = forward(block_in, block_lengths, params)
        grad_in, grads = backward(block_cot, kept, params)
        return (jax.tree.map(jnp.add, totals, grads), (result, grad_in))
    return lax.scan(one_block, zeros_init, (inputs, cots, seq_table))

def reference(tokens, lengths, w_qkv, w_out, w_up, up_bias, w_down, gains, biases, cotangent):
    block_count = DEV_ST * MICRO
    inputs = tokens.reshape(block_count, ROWS_MB, D)
    cots = cotangent.reshape(block_count, ROWS_MB, D)
    seq_table = lengths.reshape(block_count, SEQS)
    first = layer_params(0, w_qkv, w_out, w_up, up_bias, w_down, gains, biases)
    second = layer_params(1, w_qkv, w_out, w_up, up_bias, w_down, gains, biases)
    middle = lax.map(lambda block: forward(block[0], block[1], first)[0], (inputs, seq_table))
    totals_two, (outputs_two, grads_mid) = run_layer(middle, cots, seq_table, second)
    totals_one, (unused_out, grads_in) = run_layer(inputs, grads_mid, seq_table, first)
    layer_outputs = jnp.stack([middle.reshape(TOKENS, D), outputs_two.reshape(TOKENS, D)])
    input_grads = jnp.stack([grads_in.reshape(TOKENS, D), grads_mid.reshape(TOKENS, D)])
    stacked = [jnp.stack([part_one, part_two]) for part_one, part_two in zip(totals_one, totals_two)]
    return (layer_outputs, input_grads, stacked[0], stacked[1], stacked[2], stacked[3], stacked[4], stacked[6], stacked[5])
```

```python
import math

import jax
import jax.numpy as jnp
from jax import lax
from jax.sharding import PartitionSpec as P

HEADS = 17


EPSILON = 1e-05
GELU_SCALE = math.sqrt(2.0 / math.pi)
GELU_CUBIC = 0.044715


def shifted(block, axis, distance):
    devices = range(lax.axis_size(axis))
    route = [(i - distance, i) for i in devices if i - distance in devices]
    return lax.ppermute(block, axis, route)


def norm_rows(values):
    centre = values - jnp.mean(values, axis=-1, keepdims=True)
    inverse = lax.rsqrt(jnp.mean(centre * centre, axis=-1, keepdims=True) + EPSILON)
    return (centre * inverse, inverse)


def norm_back(grad_normed, normed, inverse, gain):
    scaled = grad_normed * gain
    return (
        scaled
        - jnp.mean(scaled, axis=-1, keepdims=True)
        - normed * jnp.mean(scaled * normed, axis=-1, keepdims=True)
    ) * inverse


def gelu_tanh(values):
    return (
        0.5
        * values
        * (1.0 + jnp.tanh(GELU_SCALE * (values + GELU_CUBIC * values * values * values)))
    )


def gelu_slope(values):
    tangent = jnp.tanh(GELU_SCALE * (values + GELU_CUBIC * values * values * values))
    return 0.5 * (1.0 + tangent) + 0.5 * values * (1.0 - tangent * tangent) * GELU_SCALE * (
        1.0 + 3.0 * GELU_CUBIC * values * values
    )


def contract_rows(left, right):
    return lax.dot_general(
        left, right, (((0,), (0,)), ((), ())), preferred_element_type=jnp.float32
    )


def contract_cols(left, right):
    return lax.dot_general(
        left, right, (((1,), (1,)), ((), ())), preferred_element_type=jnp.float32
    )


def make_segments(seq_lengths, row_count):
    block_count = seq_lengths.shape[0]
    block_rows = row_count // block_count
    ends = jnp.cumsum(seq_lengths.astype(jnp.int32), axis=1)
    starts = jnp.arange(block_count, dtype=jnp.int32)[:, None] * block_rows
    ends = (ends + starts).reshape(-1)
    places = jnp.arange(row_count, dtype=jnp.int32)
    segment = jnp.sum((places[:, None] >= ends[None, :]).astype(jnp.int32), axis=1)
    return (segment[:, None] == segment[None, :]) & (places[None, :] <= places[:, None])


def head_split(values):
    return values.reshape(values.shape[0], HEADS, values.shape[1] // HEADS).transpose(1, 0, 2)


def head_join(values):
    return values.transpose(1, 0, 2).reshape(values.shape[1], -1)


def batched(left, right, left_dim, right_dim):
    return lax.dot_general(
        left,
        right,
        (((left_dim,), (right_dim,)), ((0,), (0,))),
        preferred_element_type=jnp.float32,
    )


def gather_all(rows):
    over_dp = lax.all_gather(rows, "dp", axis=0, tiled=True)
    return lax.all_gather(over_dp, "tensor", axis=0, tiled=True)


def layer_forward(layer_in, allowed, params):
    w_qkv, w_out, w_up, up_bias, w_down, gains, biases = params
    row_count, model_width = layer_in.shape
    head_width = model_width // HEADS
    inflow = layer_in.astype(jnp.float32)
    normed_one, inverse_one = norm_rows(inflow)
    normal_one = (normed_one * gains[0] + biases[0]).astype(jnp.bfloat16)
    projected = jnp.dot(normal_one, w_qkv, preferred_element_type=jnp.float32)
    queries = head_split((projected[:, :model_width] + biases[1]).astype(jnp.bfloat16))
    keys_all = head_split(projected[:, model_width : 2 * model_width].astype(jnp.bfloat16))
    values_all = head_split((projected[:, 2 * model_width :] + biases[2]).astype(jnp.bfloat16))
    scores = batched(queries, keys_all, 2, 2) * head_width ** (-0.5)
    masked = jnp.where(allowed[None], scores, -jnp.inf)
    peak = jnp.max(masked, axis=-1, keepdims=True)
    raised = jnp.exp(masked - peak)
    probs_f = raised / jnp.sum(raised, axis=-1, keepdims=True)
    probs = probs_f.astype(jnp.bfloat16)
    mixed = head_join(batched(probs, values_all, 2, 1)).astype(jnp.bfloat16)
    residual = inflow + jnp.dot(mixed, w_out, preferred_element_type=jnp.float32) + biases[3]
    normed_two, inverse_two = norm_rows(residual)
    normal_two = (normed_two * gains[1] + biases[4]).astype(jnp.bfloat16)
    gathered = lax.all_gather(normal_two, "tensor", axis=0, tiled=True)
    hidden_pre = jnp.dot(gathered, w_up, preferred_element_type=jnp.float32) + up_bias
    hidden = gelu_tanh(hidden_pre).astype(jnp.bfloat16)
    branch = lax.psum_scatter(
        jnp.dot(hidden, w_down, preferred_element_type=jnp.float32).astype(jnp.bfloat16),
        "tensor",
        scatter_dimension=0,
        tiled=True,
    ).astype(jnp.float32)
    result = (residual + branch + biases[5]).astype(jnp.bfloat16)
    kept = (
        normal_one,
        normed_one,
        inverse_one,
        queries,
        keys_all,
        values_all,
        mixed,
        probs_f,
        normed_two,
        inverse_two,
        normal_two,
        hidden_pre,
    )
    return (result, kept)


def layer_backward(grad_out, kept, params):
    w_qkv, w_out, w_up, up_bias, w_down, gains, biases = params
    (
        normal_one,
        normed_one,
        inverse_one,
        queries,
        keys_all,
        values_all,
        mixed,
        probs_f,
        normed_two,
        inverse_two,
        normal_two,
        hidden_pre,
    ) = kept
    row_count, model_width = grad_out.shape
    head_width = model_width // HEADS
    grad_flow = grad_out.astype(jnp.float32)
    grad_rows = lax.all_gather(grad_out, "tensor", axis=0, tiled=True)
    grad_hidden = contract_cols(grad_rows, w_down)
    grad_pre = grad_hidden * gelu_slope(hidden_pre)
    grad_pre_b = grad_pre.astype(jnp.bfloat16)
    grad_two = lax.psum_scatter(
        contract_cols(grad_pre_b, w_up).astype(jnp.bfloat16),
        "tensor",
        scatter_dimension=0,
        tiled=True,
    ).astype(jnp.float32)
    grad_resid = grad_flow + norm_back(grad_two, normed_two, inverse_two, gains[1])
    grad_resid_b = grad_resid.astype(jnp.bfloat16)
    grad_mixed = head_split(contract_cols(grad_resid_b, w_out).astype(jnp.bfloat16))
    probs_b = probs_f.astype(jnp.bfloat16)
    grad_probs = batched(grad_mixed, values_all, 2, 2)
    grad_values = head_join(batched(probs_b, grad_mixed, 1, 1))
    centre = jnp.sum(probs_f * grad_probs, axis=-1, keepdims=True)
    grad_scores = (probs_f * (grad_probs - centre) * head_width ** (-0.5)).astype(jnp.bfloat16)
    grad_queries = head_join(batched(grad_scores, keys_all, 2, 1))
    grad_keys = head_join(batched(grad_scores, queries, 1, 1))
    grad_proj = jnp.concatenate([grad_queries, grad_keys, grad_values], axis=1).astype(jnp.bfloat16)
    grad_one = contract_cols(grad_proj, w_qkv)
    grad_in = (grad_resid + norm_back(grad_one, normed_one, inverse_one, gains[0])).astype(
        jnp.bfloat16
    )

    def feed_grads():
        inputs_all = gather_all(normal_two)
        grads_all = gather_all(grad_out)
        pre_all = jnp.dot(inputs_all, w_up, preferred_element_type=jnp.float32) + up_bias
        hidden_all = gelu_tanh(pre_all).astype(jnp.bfloat16)
        grad_all = contract_cols(grads_all, w_down) * gelu_slope(pre_all)
        return (
            contract_rows(inputs_all, grad_all.astype(jnp.bfloat16)),
            contract_rows(hidden_all, grads_all),
            jnp.sum(grad_all, axis=0),
        )

    def token_grads():
        small = jnp.stack(
            [
                jnp.sum(normed_one * grad_one, axis=0),
                jnp.sum(normed_two * grad_two, axis=0),
                jnp.sum(grad_one, axis=0),
                jnp.sum(grad_queries, axis=0),
                jnp.sum(grad_values, axis=0),
                jnp.sum(grad_resid, axis=0),
                jnp.sum(grad_two, axis=0),
                jnp.sum(grad_flow, axis=0),
            ]
        )
        return (
            contract_rows(normal_one, grad_proj),
            contract_rows(mixed, grad_resid_b),
            small,
        )

    return (grad_in, feed_grads, token_grads)


def per_device(tokens, lengths, w_qkv, w_out, w_up, up_bias, w_down, gains, biases, cotangent):
    section_index = lax.axis_index("section")
    row_count, model_width = tokens.shape
    params = (w_qkv[0], w_out[0], w_up[0], up_bias[0], w_down[0], gains[0], biases[0])
    allowed = make_segments(lengths[0], row_count)
    first_result, _ = layer_forward(tokens, allowed, params)
    arrived = shifted(first_result, "section", 1)
    layer_in = jnp.where(section_index == 0, tokens, arrived)
    result, kept = layer_forward(layer_in, allowed, params)
    first_grad, _, _ = layer_backward(cotangent, kept, params)
    grad_arrived = shifted(first_grad, "section", -1)
    grad_out = jnp.where(section_index == 1, cotangent, grad_arrived)
    grad_in, feed_grads, token_grads = layer_backward(grad_out, kept, params)

    grad_up, grad_down, grad_up_bias = feed_grads()
    grad_wqkv, grad_wout, small = token_grads()
    owners = lax.axis_size(("dp", "tensor"))
    piece = model_width // owners
    joined = jnp.concatenate([grad_wqkv, grad_wout, small.T], axis=1).astype(jnp.bfloat16)
    joined = lax.psum_scatter(
        joined.reshape(owners, piece, -1), ("dp", "tensor"), scatter_dimension=0
    ).astype(jnp.float32)
    qkv_width = grad_wqkv.shape[1]
    small = joined[:, qkv_width + model_width :].T
    return (
        result[None],
        grad_in[None],
        joined[None, :, :qkv_width],
        joined[None, :, qkv_width : qkv_width + model_width],
        small[None, :2],
        small[None, 2:],
        grad_up[None],
        grad_up_bias[None],
        grad_down[None],
    )


def solution(mesh):
    in_specs = (
        P(("dp", "tensor"), None),
        P(("dp", "tensor"), None, None),
        P("section", None, None),
        P("section", None, None),
        P("section", None, "tensor"),
        P("section", "tensor"),
        P("section", "tensor", None),
        P("section", None, None),
        P("section", None, None),
        P(("dp", "tensor"), None),
    )
    out_specs = (
        P("section", ("dp", "tensor"), None),
        P("section", ("dp", "tensor"), None),
        P("section", ("dp", "tensor"), None),
        P("section", ("dp", "tensor"), None),
        P("section", None, ("dp", "tensor")),
        P("section", None, ("dp", "tensor")),
        P("section", None, "tensor"),
        P("section", "tensor"),
        P("section", "tensor", None),
    )
    return jax.shard_map(
        per_device, mesh=mesh, in_specs=in_specs, out_specs=out_specs, check_vma=False
    )
```

```python
import functools
import math

import jax
import jax.numpy as jnp
from jax import lax
from jax.experimental import pallas as pl
from jax.experimental.pallas import tpu as pltpu
from jax.sharding import PartitionSpec as P

HEADS = 17


EPSILON = 1e-05
GELU_SCALE = math.sqrt(2.0 / math.pi)
GELU_CUBIC = 0.044715


def shifted(block, axis, distance):
    devices = range(lax.axis_size(axis))
    route = [(i - distance, i) for i in devices if i - distance in devices]
    return lax.ppermute(block, axis, route)


def norm_rows(values):
    centre = values - jnp.mean(values, axis=-1, keepdims=True)
    inverse = lax.rsqrt(jnp.mean(centre * centre, axis=-1, keepdims=True) + EPSILON)
    return (centre * inverse, inverse)


def norm_back(grad_normed, normed, inverse, gain):
    scaled = grad_normed * gain
    return (
        scaled
        - jnp.mean(scaled, axis=-1, keepdims=True)
        - normed * jnp.mean(scaled * normed, axis=-1, keepdims=True)
    ) * inverse


def gelu_tanh(values):
    return (
        0.5
        * values
        * (1.0 + jnp.tanh(GELU_SCALE * (values + GELU_CUBIC * values * values * values)))
    )


def gelu_slope(values):
    tangent = jnp.tanh(GELU_SCALE * (values + GELU_CUBIC * values * values * values))
    return 0.5 * (1.0 + tangent) + 0.5 * values * (1.0 - tangent * tangent) * GELU_SCALE * (
        1.0 + 3.0 * GELU_CUBIC * values * values
    )


def contract_rows(left, right):
    return lax.dot_general(
        left, right, (((0,), (0,)), ((), ())), preferred_element_type=jnp.float32
    )


def contract_cols(left, right):
    return lax.dot_general(
        left, right, (((1,), (1,)), ((), ())), preferred_element_type=jnp.float32
    )


def make_segments(seq_lengths, row_count):
    block_count = seq_lengths.shape[0]
    block_rows = row_count // block_count
    ends = jnp.cumsum(seq_lengths.astype(jnp.int32), axis=1)
    starts = jnp.arange(block_count, dtype=jnp.int32)[:, None] * block_rows
    ends = (ends + starts).reshape(-1)
    places = jnp.arange(row_count, dtype=jnp.int32)
    segment = jnp.sum((places[:, None] >= ends[None, :]).astype(jnp.int32), axis=1)
    return (segment[:, None] == segment[None, :]) & (places[None, :] <= places[:, None])


def head_split(values):
    return values.reshape(values.shape[0], HEADS, values.shape[1] // HEADS).transpose(1, 0, 2)


def head_join(values):
    return values.transpose(1, 0, 2).reshape(values.shape[1], -1)


def batched(left, right, left_dim, right_dim):
    return lax.dot_general(
        left,
        right,
        (((left_dim,), (right_dim,)), ((0,), (0,))),
        preferred_element_type=jnp.float32,
    )


def greet(partner, peers):
    barrier = pltpu.get_barrier_semaphore()
    for place in [partner] + peers:
        pl.semaphore_signal(
            barrier,
            inc=1,
            device_id={"tensor": place},
            device_id_type=pl.DeviceIdType.MESH,
        )
    pl.semaphore_wait(barrier, 1 + len(peers))


def send(source, target, send_sem, recv_sem, place):
    copy = pltpu.make_async_remote_copy(
        src_ref=source,
        dst_ref=target,
        send_sem=send_sem,
        recv_sem=recv_sem,
        device_id={"tensor": place},
        device_id_type=pl.DeviceIdType.MESH,
    )
    copy.start()
    return copy


def gather_kernel(chips, rows, own_ref, out_ref, send_sem, recv_sem):
    me = lax.axis_index("tensor")
    core = lax.rem(me, 2)
    chip = me // 2
    partner = me + 1 - 2 * core
    peers = [lax.rem(chip + k, chips) * 2 + core for k in range(1, chips)]
    greet(partner, peers)

    def block(index):
        return out_ref.at[pl.ds(pl.multiple_of(index * rows, rows), rows)]

    across = [
        send(own_ref, block(me), send_sem.at[k], recv_sem.at[k], peer)
        for k, peer in enumerate(peers)
    ]
    beside = [send(own_ref, block(me), send_sem.at[chips - 1], recv_sem.at[chips - 1], partner)]
    out_ref[pl.ds(pl.multiple_of(me * rows, rows), rows)] = own_ref[...]
    for k, copy in enumerate(across):
        copy.wait_recv()
        origin = block(lax.rem(chip + chips - 1 - k, chips) * 2 + core)
        beside.append(send(origin, origin, send_sem.at[chips + k], recv_sem.at[chips + k], partner))
    for copy in across:
        copy.wait_send()
    for copy in beside:
        copy.wait()


def gather_rows(own):
    chips = lax.axis_size("tensor") // 2
    rows, width = own.shape
    return pl.pallas_call(
        functools.partial(gather_kernel, chips, rows),
        out_shape=jax.ShapeDtypeStruct((2 * chips * rows, width), own.dtype),
        in_specs=[pl.BlockSpec(memory_space=pltpu.VMEM)],
        out_specs=pl.BlockSpec(memory_space=pltpu.VMEM),
        scratch_shapes=[
            pltpu.SemaphoreType.DMA((2 * chips - 1,)),
            pltpu.SemaphoreType.DMA((2 * chips - 1,)),
        ],
        compiler_params=pltpu.CompilerParams(collective_id=0, has_side_effects=True),
    )(own)


def scatter_kernel(
    chips,
    rows,
    part_ref,
    out_ref,
    beside_buf,
    stage_buf,
    across_buf,
    beside_send,
    beside_recv,
    across_send,
    across_recv,
):
    me = lax.axis_index("tensor")
    core = lax.rem(me, 2)
    chip = me // 2
    partner = me + 1 - 2 * core
    targets = [lax.rem(chip + 1 + k, chips) for k in range(chips)]
    peers = [target * 2 + core for target in targets[:-1]]
    greet(partner, peers)

    def span(index):
        return pl.ds(pl.multiple_of(index * rows, rows), rows)

    beside = [
        send(
            part_ref.at[span(target * 2 + 1 - core)],
            beside_buf.at[k],
            beside_send.at[k],
            beside_recv.at[k],
            partner,
        )
        for k, target in enumerate(targets)
    ]
    across = []
    for k, target in enumerate(targets):
        beside[k].wait_recv()
        total = part_ref[span(target * 2 + core)].astype(jnp.float32)
        total = total + beside_buf[k].astype(jnp.float32)
        if k < chips - 1:
            stage_buf[k] = total.astype(stage_buf.dtype)
            across.append(
                send(
                    stage_buf.at[k],
                    across_buf.at[k],
                    across_send.at[k],
                    across_recv.at[k],
                    peers[k],
                )
            )
        else:
            out_ref[...] = total
    for k, copy in enumerate(across):
        copy.wait_recv()
        out_ref[...] += across_buf[k].astype(jnp.float32)
    for copy in beside + across:
        copy.wait_send()


def scatter_rows(parts):
    chips = lax.axis_size("tensor") // 2
    rows, width = parts.shape[0] // (2 * chips), parts.shape[1]
    hops = max(chips - 1, 1)
    return pl.pallas_call(
        functools.partial(scatter_kernel, chips, rows),
        out_shape=jax.ShapeDtypeStruct((rows, width), jnp.float32),
        in_specs=[pl.BlockSpec(memory_space=pltpu.VMEM)],
        out_specs=pl.BlockSpec(memory_space=pltpu.VMEM),
        scratch_shapes=[
            pltpu.VMEM((chips, rows, width), parts.dtype),
            pltpu.VMEM((hops, rows, width), parts.dtype),
            pltpu.VMEM((hops, rows, width), parts.dtype),
            pltpu.SemaphoreType.DMA((chips,)),
            pltpu.SemaphoreType.DMA((chips,)),
            pltpu.SemaphoreType.DMA((hops,)),
            pltpu.SemaphoreType.DMA((hops,)),
        ],
        compiler_params=pltpu.CompilerParams(collective_id=1, has_side_effects=True),
    )(parts)


def gather_all(rows):
    over_dp = lax.all_gather(rows, "dp", axis=0, tiled=True)
    return lax.all_gather(over_dp, "tensor", axis=0, tiled=True)


def layer_forward(layer_in, allowed, params):
    w_qkv, w_out, w_up, up_bias, w_down, gains, biases = params
    row_count, model_width = layer_in.shape
    head_width = model_width // HEADS
    inflow = layer_in.astype(jnp.float32)
    normed_one, inverse_one = norm_rows(inflow)
    normal_one = (normed_one * gains[0] + biases[0]).astype(jnp.bfloat16)
    projected = jnp.dot(normal_one, w_qkv, preferred_element_type=jnp.float32)
    queries = head_split((projected[:, :model_width] + biases[1]).astype(jnp.bfloat16))
    keys_all = head_split(projected[:, model_width : 2 * model_width].astype(jnp.bfloat16))
    values_all = head_split((projected[:, 2 * model_width :] + biases[2]).astype(jnp.bfloat16))
    scores = batched(queries, keys_all, 2, 2) * head_width ** (-0.5)
    masked = jnp.where(allowed[None], scores, -jnp.inf)
    peak = jnp.max(masked, axis=-1, keepdims=True)
    raised = jnp.exp(masked - peak)
    probs_f = raised / jnp.sum(raised, axis=-1, keepdims=True)
    probs = probs_f.astype(jnp.bfloat16)
    mixed = head_join(batched(probs, values_all, 2, 1)).astype(jnp.bfloat16)
    residual = inflow + jnp.dot(mixed, w_out, preferred_element_type=jnp.float32) + biases[3]
    normed_two, inverse_two = norm_rows(residual)
    normal_two = (normed_two * gains[1] + biases[4]).astype(jnp.bfloat16)
    gathered = gather_rows(normal_two)
    hidden_pre = jnp.dot(gathered, w_up, preferred_element_type=jnp.float32) + up_bias
    hidden = gelu_tanh(hidden_pre).astype(jnp.bfloat16)
    branch = scatter_rows(
        jnp.dot(hidden, w_down, preferred_element_type=jnp.float32).astype(jnp.bfloat16)
    )
    result = (residual + branch + biases[5]).astype(jnp.bfloat16)
    kept = (
        normal_one,
        normed_one,
        inverse_one,
        queries,
        keys_all,
        values_all,
        mixed,
        probs_f,
        normed_two,
        inverse_two,
        normal_two,
        hidden_pre,
    )
    return (result, kept)


def layer_backward(grad_out, kept, params):
    w_qkv, w_out, w_up, up_bias, w_down, gains, biases = params
    (
        normal_one,
        normed_one,
        inverse_one,
        queries,
        keys_all,
        values_all,
        mixed,
        probs_f,
        normed_two,
        inverse_two,
        normal_two,
        hidden_pre,
    ) = kept
    row_count, model_width = grad_out.shape
    head_width = model_width // HEADS
    grad_flow = grad_out.astype(jnp.float32)
    grad_rows = gather_rows(grad_out)
    grad_hidden = contract_cols(grad_rows, w_down)
    grad_pre = grad_hidden * gelu_slope(hidden_pre)
    grad_pre_b = grad_pre.astype(jnp.bfloat16)
    grad_two = scatter_rows(contract_cols(grad_pre_b, w_up).astype(jnp.bfloat16))
    grad_resid = grad_flow + norm_back(grad_two, normed_two, inverse_two, gains[1])
    grad_resid_b = grad_resid.astype(jnp.bfloat16)
    grad_mixed = head_split(contract_cols(grad_resid_b, w_out).astype(jnp.bfloat16))
    probs_b = probs_f.astype(jnp.bfloat16)
    grad_probs = batched(grad_mixed, values_all, 2, 2)
    grad_values = head_join(batched(probs_b, grad_mixed, 1, 1))
    centre = jnp.sum(probs_f * grad_probs, axis=-1, keepdims=True)
    grad_scores = (probs_f * (grad_probs - centre) * head_width ** (-0.5)).astype(jnp.bfloat16)
    grad_queries = head_join(batched(grad_scores, keys_all, 2, 1))
    grad_keys = head_join(batched(grad_scores, queries, 1, 1))
    grad_proj = jnp.concatenate([grad_queries, grad_keys, grad_values], axis=1).astype(jnp.bfloat16)
    grad_one = contract_cols(grad_proj, w_qkv)
    grad_in = (grad_resid + norm_back(grad_one, normed_one, inverse_one, gains[0])).astype(
        jnp.bfloat16
    )

    def feed_grads():
        inputs_all = gather_all(normal_two)
        grads_all = gather_all(grad_out)
        pre_all = jnp.dot(inputs_all, w_up, preferred_element_type=jnp.float32) + up_bias
        hidden_all = gelu_tanh(pre_all).astype(jnp.bfloat16)
        grad_all = contract_cols(grads_all, w_down) * gelu_slope(pre_all)
        return (
            contract_rows(inputs_all, grad_all.astype(jnp.bfloat16)),
            contract_rows(hidden_all, grads_all),
            jnp.sum(grad_all, axis=0),
        )

    def token_grads():
        small = jnp.stack(
            [
                jnp.sum(normed_one * grad_one, axis=0),
                jnp.sum(normed_two * grad_two, axis=0),
                jnp.sum(grad_one, axis=0),
                jnp.sum(grad_queries, axis=0),
                jnp.sum(grad_values, axis=0),
                jnp.sum(grad_resid, axis=0),
                jnp.sum(grad_two, axis=0),
                jnp.sum(grad_flow, axis=0),
            ]
        )
        return (
            contract_rows(normal_one, grad_proj),
            contract_rows(mixed, grad_resid_b),
            small,
        )

    return (grad_in, feed_grads, token_grads)


def per_device(tokens, lengths, w_qkv, w_out, w_up, up_bias, w_down, gains, biases, cotangent):
    section_index = lax.axis_index("section")
    row_count, model_width = tokens.shape
    params = (w_qkv[0], w_out[0], w_up[0], up_bias[0], w_down[0], gains[0], biases[0])
    allowed = make_segments(lengths[0], row_count)
    first_result, _ = layer_forward(tokens, allowed, params)
    arrived = shifted(first_result, "section", 1)
    layer_in = jnp.where(section_index == 0, tokens, arrived)
    result, kept = layer_forward(layer_in, allowed, params)
    first_grad, _, _ = layer_backward(cotangent, kept, params)
    grad_arrived = shifted(first_grad, "section", -1)
    grad_out = jnp.where(section_index == 1, cotangent, grad_arrived)
    grad_in, feed_grads, token_grads = layer_backward(grad_out, kept, params)

    grad_up, grad_down, grad_up_bias = feed_grads()
    grad_wqkv, grad_wout, small = token_grads()
    owners = lax.axis_size(("dp", "tensor"))
    piece = model_width // owners
    joined = jnp.concatenate([grad_wqkv, grad_wout, small.T], axis=1).astype(jnp.bfloat16)
    joined = lax.psum_scatter(
        joined.reshape(owners, piece, -1), ("dp", "tensor"), scatter_dimension=0
    ).astype(jnp.float32)
    qkv_width = grad_wqkv.shape[1]
    small = joined[:, qkv_width + model_width :].T
    return (
        result[None],
        grad_in[None],
        joined[None, :, :qkv_width],
        joined[None, :, qkv_width : qkv_width + model_width],
        small[None, :2],
        small[None, 2:],
        grad_up[None],
        grad_up_bias[None],
        grad_down[None],
    )


def solution(mesh):
    in_specs = (
        P(("dp", "tensor"), None),
        P(("dp", "tensor"), None, None),
        P("section", None, None),
        P("section", None, None),
        P("section", None, "tensor"),
        P("section", "tensor"),
        P("section", "tensor", None),
        P("section", None, None),
        P("section", None, None),
        P(("dp", "tensor"), None),
    )
    out_specs = (
        P("section", ("dp", "tensor"), None),
        P("section", ("dp", "tensor"), None),
        P("section", ("dp", "tensor"), None),
        P("section", ("dp", "tensor"), None),
        P("section", None, ("dp", "tensor")),
        P("section", None, ("dp", "tensor")),
        P("section", None, "tensor"),
        P("section", "tensor"),
        P("section", "tensor", None),
    )
    return jax.shard_map(
        per_device, mesh=mesh, in_specs=in_specs, out_specs=out_specs, check_vma=False
    )
```

```python
import functools
import math

import jax
import jax.numpy as jnp
from jax import lax
from jax.experimental import pallas as pl
from jax.experimental.pallas import tpu as pltpu
from jax.sharding import PartitionSpec as P

HEADS = 17


EPSILON = 1e-05
GELU_SCALE = math.sqrt(2.0 / math.pi)
GELU_CUBIC = 0.044715


def shifted(block, axis, distance):
    devices = range(lax.axis_size(axis))
    route = [(i - distance, i) for i in devices if i - distance in devices]
    return lax.ppermute(block, axis, route)


def norm_rows(values):
    centre = values - jnp.mean(values, axis=-1, keepdims=True)
    inverse = lax.rsqrt(jnp.mean(centre * centre, axis=-1, keepdims=True) + EPSILON)
    return (centre * inverse, inverse)


def norm_back(grad_normed, normed, inverse, gain):
    scaled = grad_normed * gain
    return (
        scaled
        - jnp.mean(scaled, axis=-1, keepdims=True)
        - normed * jnp.mean(scaled * normed, axis=-1, keepdims=True)
    ) * inverse


def gelu_tanh(values):
    return (
        0.5
        * values
        * (1.0 + jnp.tanh(GELU_SCALE * (values + GELU_CUBIC * values * values * values)))
    )


def gelu_slope(values):
    tangent = jnp.tanh(GELU_SCALE * (values + GELU_CUBIC * values * values * values))
    return 0.5 * (1.0 + tangent) + 0.5 * values * (1.0 - tangent * tangent) * GELU_SCALE * (
        1.0 + 3.0 * GELU_CUBIC * values * values
    )


def contract_rows(left, right):
    return lax.dot_general(
        left, right, (((0,), (0,)), ((), ())), preferred_element_type=jnp.float32
    )


def contract_cols(left, right):
    return lax.dot_general(
        left, right, (((1,), (1,)), ((), ())), preferred_element_type=jnp.float32
    )


def make_segments(seq_lengths, row_count):
    block_count = seq_lengths.shape[0]
    block_rows = row_count // block_count
    ends = jnp.cumsum(seq_lengths.astype(jnp.int32), axis=1)
    starts = jnp.arange(block_count, dtype=jnp.int32)[:, None] * block_rows
    ends = (ends + starts).reshape(-1)
    places = jnp.arange(row_count, dtype=jnp.int32)
    segment = jnp.sum((places[:, None] >= ends[None, :]).astype(jnp.int32), axis=1)
    return (segment[:, None] == segment[None, :]) & (places[None, :] <= places[:, None])


def head_split(values):
    return values.reshape(values.shape[0], HEADS, values.shape[1] // HEADS).transpose(1, 0, 2)


def head_join(values):
    return values.transpose(1, 0, 2).reshape(values.shape[1], -1)


def batched(left, right, left_dim, right_dim):
    return lax.dot_general(
        left,
        right,
        (((left_dim,), (right_dim,)), ((0,), (0,))),
        preferred_element_type=jnp.float32,
    )


def greet(partner, peers):
    barrier = pltpu.get_barrier_semaphore()
    for place in [partner] + peers:
        pl.semaphore_signal(
            barrier,
            inc=1,
            device_id={"tensor": place},
            device_id_type=pl.DeviceIdType.MESH,
        )
    pl.semaphore_wait(barrier, 1 + len(peers))


def send(source, target, send_sem, recv_sem, place):
    copy = pltpu.make_async_remote_copy(
        src_ref=source,
        dst_ref=target,
        send_sem=send_sem,
        recv_sem=recv_sem,
        device_id={"tensor": place},
        device_id_type=pl.DeviceIdType.MESH,
    )
    copy.start()
    return copy


def gather_kernel(chips, rows, own_ref, out_ref, send_sem, recv_sem):
    me = lax.axis_index("tensor")
    core = lax.rem(me, 2)
    chip = me // 2
    partner = me + 1 - 2 * core
    peers = [lax.rem(chip + k, chips) * 2 + core for k in range(1, chips)]
    greet(partner, peers)

    def block(index):
        return out_ref.at[pl.ds(pl.multiple_of(index * rows, rows), rows)]

    across = [
        send(own_ref, block(me), send_sem.at[k], recv_sem.at[k], peer)
        for k, peer in enumerate(peers)
    ]
    beside = [send(own_ref, block(me), send_sem.at[chips - 1], recv_sem.at[chips - 1], partner)]
    out_ref[pl.ds(pl.multiple_of(me * rows, rows), rows)] = own_ref[...]
    for k, copy in enumerate(across):
        copy.wait_recv()
        origin = block(lax.rem(chip + chips - 1 - k, chips) * 2 + core)
        beside.append(send(origin, origin, send_sem.at[chips + k], recv_sem.at[chips + k], partner))
    for copy in across:
        copy.wait_send()
    for copy in beside:
        copy.wait()


def gather_rows(own, call=0):
    chips = lax.axis_size("tensor") // 2
    rows, width = own.shape
    return pl.pallas_call(
        functools.partial(gather_kernel, chips, rows),
        out_shape=jax.ShapeDtypeStruct((2 * chips * rows, width), own.dtype),
        in_specs=[pl.BlockSpec(memory_space=pltpu.VMEM)],
        out_specs=pl.BlockSpec(memory_space=pltpu.VMEM),
        scratch_shapes=[
            pltpu.SemaphoreType.DMA((2 * chips - 1,)),
            pltpu.SemaphoreType.DMA((2 * chips - 1,)),
        ],
        compiler_params=pltpu.CompilerParams(collective_id=call, has_side_effects=True),
    )(own)


def scatter_kernel(
    chips,
    rows,
    part_ref,
    out_ref,
    beside_buf,
    stage_buf,
    across_buf,
    beside_send,
    beside_recv,
    across_send,
    across_recv,
):
    me = lax.axis_index("tensor")
    core = lax.rem(me, 2)
    chip = me // 2
    partner = me + 1 - 2 * core
    targets = [lax.rem(chip + 1 + k, chips) for k in range(chips)]
    peers = [target * 2 + core for target in targets[:-1]]
    greet(partner, peers)

    def span(index):
        return pl.ds(pl.multiple_of(index * rows, rows), rows)

    beside = [
        send(
            part_ref.at[span(target * 2 + 1 - core)],
            beside_buf.at[k],
            beside_send.at[k],
            beside_recv.at[k],
            partner,
        )
        for k, target in enumerate(targets)
    ]
    across = []
    for k, target in enumerate(targets):
        beside[k].wait_recv()
        total = part_ref[span(target * 2 + core)].astype(jnp.float32)
        total = total + beside_buf[k].astype(jnp.float32)
        if k < chips - 1:
            stage_buf[k] = total.astype(stage_buf.dtype)
            across.append(
                send(
                    stage_buf.at[k],
                    across_buf.at[k],
                    across_send.at[k],
                    across_recv.at[k],
                    peers[k],
                )
            )
        else:
            out_ref[...] = total
    for k, copy in enumerate(across):
        copy.wait_recv()
        out_ref[...] += across_buf[k].astype(jnp.float32)
    for copy in beside + across:
        copy.wait_send()


def scatter_rows(parts):
    chips = lax.axis_size("tensor") // 2
    rows, width = parts.shape[0] // (2 * chips), parts.shape[1]
    hops = max(chips - 1, 1)
    return pl.pallas_call(
        functools.partial(scatter_kernel, chips, rows),
        out_shape=jax.ShapeDtypeStruct((rows, width), jnp.float32),
        in_specs=[pl.BlockSpec(memory_space=pltpu.VMEM)],
        out_specs=pl.BlockSpec(memory_space=pltpu.VMEM),
        scratch_shapes=[
            pltpu.VMEM((chips, rows, width), parts.dtype),
            pltpu.VMEM((hops, rows, width), parts.dtype),
            pltpu.VMEM((hops, rows, width), parts.dtype),
            pltpu.SemaphoreType.DMA((chips,)),
            pltpu.SemaphoreType.DMA((chips,)),
            pltpu.SemaphoreType.DMA((hops,)),
            pltpu.SemaphoreType.DMA((hops,)),
        ],
        compiler_params=pltpu.CompilerParams(collective_id=1, has_side_effects=True),
    )(parts)


def layer_forward(layer_in, allowed, params):
    w_qkv, w_out, w_up, up_bias, w_down, gains, biases = params
    row_count, model_width = layer_in.shape
    head_width = model_width // HEADS
    inflow = layer_in.astype(jnp.float32)
    normed_one, inverse_one = norm_rows(inflow)
    normal_one = (normed_one * gains[0] + biases[0]).astype(jnp.bfloat16)
    projected = jnp.dot(normal_one, w_qkv, preferred_element_type=jnp.float32)
    queries = head_split((projected[:, :model_width] + biases[1]).astype(jnp.bfloat16))
    keys_all = head_split(projected[:, model_width : 2 * model_width].astype(jnp.bfloat16))
    values_all = head_split((projected[:, 2 * model_width :] + biases[2]).astype(jnp.bfloat16))
    scores = batched(queries, keys_all, 2, 2) * head_width ** (-0.5)
    masked = jnp.where(allowed[None], scores, -jnp.inf)
    peak = jnp.max(masked, axis=-1, keepdims=True)
    raised = jnp.exp(masked - peak)
    probs_f = raised / jnp.sum(raised, axis=-1, keepdims=True)
    probs = probs_f.astype(jnp.bfloat16)
    mixed = head_join(batched(probs, values_all, 2, 1)).astype(jnp.bfloat16)
    residual = inflow + jnp.dot(mixed, w_out, preferred_element_type=jnp.float32) + biases[3]
    normed_two, inverse_two = norm_rows(residual)
    normal_two = (normed_two * gains[1] + biases[4]).astype(jnp.bfloat16)
    gathered = gather_rows(normal_two)
    hidden_pre = jnp.dot(gathered, w_up, preferred_element_type=jnp.float32) + up_bias
    hidden = gelu_tanh(hidden_pre).astype(jnp.bfloat16)
    branch = scatter_rows(
        jnp.dot(hidden, w_down, preferred_element_type=jnp.float32).astype(jnp.bfloat16)
    )
    result = (residual + branch + biases[5]).astype(jnp.bfloat16)
    kept = (
        normal_one,
        normed_one,
        inverse_one,
        queries,
        keys_all,
        values_all,
        mixed,
        probs_f,
        normed_two,
        inverse_two,
        normal_two,
        hidden_pre,
    )
    return (result, kept)


def layer_backward(grad_out, kept, params):
    w_qkv, w_out, w_up, up_bias, w_down, gains, biases = params
    (
        normal_one,
        normed_one,
        inverse_one,
        queries,
        keys_all,
        values_all,
        mixed,
        probs_f,
        normed_two,
        inverse_two,
        normal_two,
        hidden_pre,
    ) = kept
    row_count, model_width = grad_out.shape
    head_width = model_width // HEADS
    grad_flow = grad_out.astype(jnp.float32)
    grad_rows = gather_rows(grad_out)
    grad_hidden = contract_cols(grad_rows, w_down)
    grad_pre = grad_hidden * gelu_slope(hidden_pre)
    grad_pre_b = grad_pre.astype(jnp.bfloat16)
    grad_two = scatter_rows(contract_cols(grad_pre_b, w_up).astype(jnp.bfloat16))
    grad_resid = grad_flow + norm_back(grad_two, normed_two, inverse_two, gains[1])
    grad_resid_b = grad_resid.astype(jnp.bfloat16)
    grad_mixed = head_split(contract_cols(grad_resid_b, w_out).astype(jnp.bfloat16))
    probs_b = probs_f.astype(jnp.bfloat16)
    grad_probs = batched(grad_mixed, values_all, 2, 2)
    grad_values = head_join(batched(probs_b, grad_mixed, 1, 1))
    centre = jnp.sum(probs_f * grad_probs, axis=-1, keepdims=True)
    grad_scores = (probs_f * (grad_probs - centre) * head_width ** (-0.5)).astype(jnp.bfloat16)
    grad_queries = head_join(batched(grad_scores, keys_all, 2, 1))
    grad_keys = head_join(batched(grad_scores, queries, 1, 1))
    grad_proj = jnp.concatenate([grad_queries, grad_keys, grad_values], axis=1).astype(jnp.bfloat16)
    grad_one = contract_cols(grad_proj, w_qkv)
    grad_in = (grad_resid + norm_back(grad_one, normed_one, inverse_one, gains[0])).astype(
        jnp.bfloat16
    )

    def feed_grads(ready):
        inputs_dp = lax.all_gather(normal_two, "dp", axis=0, tiled=True)
        grads_dp = lax.all_gather(grad_out, "dp", axis=0, tiled=True)
        inputs_dp, grads_dp, ready = lax.optimization_barrier((inputs_dp, grads_dp, ready))
        inputs_all = gather_rows(inputs_dp, 2)
        grads_all = gather_rows(grads_dp, 2)
        pre_all = jnp.dot(inputs_all, w_up, preferred_element_type=jnp.float32) + up_bias
        hidden_all = gelu_tanh(pre_all).astype(jnp.bfloat16)
        grad_all = contract_cols(grads_all, w_down) * gelu_slope(pre_all)
        return (
            contract_rows(inputs_all, grad_all.astype(jnp.bfloat16)),
            contract_rows(hidden_all, grads_all),
            jnp.sum(grad_all, axis=0),
            ready,
        )

    def token_grads():
        small = jnp.stack(
            [
                jnp.sum(normed_one * grad_one, axis=0),
                jnp.sum(normed_two * grad_two, axis=0),
                jnp.sum(grad_one, axis=0),
                jnp.sum(grad_queries, axis=0),
                jnp.sum(grad_values, axis=0),
                jnp.sum(grad_resid, axis=0),
                jnp.sum(grad_two, axis=0),
                jnp.sum(grad_flow, axis=0),
            ]
        )
        return (
            contract_rows(normal_one, grad_proj),
            contract_rows(mixed, grad_resid_b),
            small,
        )

    return (grad_in, feed_grads, token_grads)


def per_device(tokens, lengths, w_qkv, w_out, w_up, up_bias, w_down, gains, biases, cotangent):
    section_index = lax.axis_index("section")
    row_count, model_width = tokens.shape
    params = (w_qkv[0], w_out[0], w_up[0], up_bias[0], w_down[0], gains[0], biases[0])
    allowed = make_segments(lengths[0], row_count)
    first_result, _ = layer_forward(tokens, allowed, params)
    arrived = shifted(first_result, "section", 1)
    layer_in = jnp.where(section_index == 0, tokens, arrived)
    result, kept = layer_forward(layer_in, allowed, params)
    first_grad, _, _ = layer_backward(cotangent, kept, params)
    grad_arrived = shifted(first_grad, "section", -1)
    grad_out = jnp.where(section_index == 1, cotangent, grad_arrived)
    grad_in, feed_grads, token_grads = layer_backward(grad_out, kept, params)

    grad_wqkv, grad_wout, small = token_grads()
    owners = lax.axis_size(("dp", "tensor"))
    piece = model_width // owners

    def scatter_all(parts):
        return lax.psum_scatter(parts, ("dp", "tensor"), scatter_dimension=0).astype(jnp.float32)

    grad_wout = scatter_all(grad_wout.astype(jnp.bfloat16).reshape(owners, piece, -1))
    qkv_width = grad_wqkv.shape[1]
    joined = jnp.concatenate([grad_wqkv.astype(jnp.bfloat16), small.T.astype(jnp.bfloat16)], axis=1)
    joined = joined.reshape(owners, piece, -1)
    grad_up, grad_down, grad_up_bias, joined = feed_grads(joined)
    joined = scatter_all(joined)
    grad_wqkv, small = joined[:, :qkv_width], joined[:, qkv_width:].T
    return (
        result[None],
        grad_in[None],
        grad_wqkv[None],
        grad_wout[None],
        small[None, :2],
        small[None, 2:],
        grad_up[None],
        grad_up_bias[None],
        grad_down[None],
    )


def solution(mesh):
    in_specs = (
        P(("dp", "tensor"), None),
        P(("dp", "tensor"), None, None),
        P("section", None, None),
        P("section", None, None),
        P("section", None, "tensor"),
        P("section", "tensor"),
        P("section", "tensor", None),
        P("section", None, None),
        P("section", None, None),
        P(("dp", "tensor"), None),
    )
    out_specs = (
        P("section", ("dp", "tensor"), None),
        P("section", ("dp", "tensor"), None),
        P("section", ("dp", "tensor"), None),
        P("section", ("dp", "tensor"), None),
        P("section", None, ("dp", "tensor")),
        P("section", None, ("dp", "tensor")),
        P("section", None, "tensor"),
        P("section", "tensor"),
        P("section", "tensor", None),
    )
    return jax.shard_map(
        per_device, mesh=mesh, in_specs=in_specs, out_specs=out_specs, check_vma=False
    )
```
